32 devices in a mesh: seq: 8 (over y, x, core), sub: 4 (over z).
Axes of the slice: x: 2, y: 2, z: 4, core: 2. Of those that a mesh axis runs over, the one named last changes fastest.
Arguments:
- video: bfloat16 [4096, 1536], P(('seq', 'sub')), may hold values from -6 to 6
- conditioning: bfloat16 [5, 1024], replicated, may hold values from -6 to 6
- captions: bfloat16 [1280, 4096], P('sub'), may hold values from -6 to 6
- clip_lengths: int32 [5], replicated, may hold values from 1 to 2048, 4096 in all
- cap_lengths: int32 [5], replicated, may hold values from 64 to 256, as said below
- positions: int32 [4096, 3], P(('seq', 'sub')), may hold values from 0 to 63
- ada_weight: bfloat16 [1024, 6144], P(('seq', 'sub')), may hold values from -0.1875 to 0.1875
- ada_bias: bfloat16 [6144], P(('seq', 'sub')), may hold values from -3 to 3
- query_weight: bfloat16 [1536, 1536], P(('seq', 'sub')), may hold values from -0.15625 to 0.15625
- key_weight: bfloat16 [1536, 1536], P(('seq', 'sub')), may hold values from -0.15625 to 0.15625
- value_weight: bfloat16 [1536, 1536], P(('seq', 'sub')), may hold values from -0.15625 to 0.15625
- out_weight: bfloat16 [1536, 1536], P(('seq', 'sub')), may hold values from -0.15625 to 0.15625
- text_key_weight: bfloat16 [4096, 1536], P(('seq', 'sub')), may hold values from -0.09375 to 0.09375
- text_value_weight: bfloat16 [4096, 1536], P(('seq', 'sub')), may hold values from -0.09375 to 0.09375
- gate_weight: bfloat16 [1536, 4096], P(('seq', 'sub')), may hold values from -0.15625 to 0.15625
- up_weight: bfloat16 [1536, 4096], P(('seq', 'sub')), may hold values from -0.15625 to 0.15625
- down_weight: bfloat16 [4096, 1536], P(('seq', 'sub')), may hold values from -0.09375 to 0.09375
- attn_gain: bfloat16 [1536], P(('seq', 'sub')), may hold values from 0.5 to 1.5
- query_gain: bfloat16 [1536], P(('seq', 'sub')), may hold values from 0.5 to 1.5
- key_gain: bfloat16 [1536], P(('seq', 'sub')), may hold values from 0.5 to 1.5
- text_key_gain: bfloat16 [1536], P(('seq', 'sub')), may hold values from 0.5 to 1.5
- attn_out_gain: bfloat16 [1536], P(('seq', 'sub')), may hold values from 0.5 to 1.5
- ffn_gain: bfloat16 [1536], P(('seq', 'sub')), may hold values from 0.5 to 1.5
- ffn_out_gain: bfloat16 [1536], P(('seq', 'sub')), may hold values from 0.5 to 1.5
- cross_gate: bfloat16 [24], replicated, may hold values from -1.5 to 1.5
- cotangent: bfloat16 [4096, 1536], P(('seq', 'sub')), may hold values from -6 to 6
Outputs:
- block_out: bfloat16 [4096, 1536], P(('seq', 'sub'))
- video_grad: float32 [4096, 1536], P(('seq', 'sub'))
- caption_grad: float32 [1280, 4096], P('sub')
- cond_grad: float32 [5, 1024], replicated
- ada_weight_grad: float32 [1024, 6144], P(('seq', 'sub'))
- ada_bias_grad: float32 [6144], P(('seq', 'sub'))
- query_weight_grad: float32 [1536, 1536], P(('seq', 'sub'))
- key_weight_grad: float32 [1536, 1536], P(('seq', 'sub'))
- value_weight_grad: float32 [1536, 1536], P(('seq', 'sub'))
- out_weight_grad: float32 [1536, 1536], P(('seq', 'sub'))
- text_key_weight_grad: float32 [4096, 1536], P(('seq', 'sub'))
- text_value_weight_grad: float32 [4096, 1536], P(('seq', 'sub'))
- gate_weight_grad: float32 [1536, 4096], P(('seq', 'sub'))
- up_weight_grad: float32 [1536, 4096], P(('seq', 'sub'))
- down_weight_grad: float32 [4096, 1536], P(('seq', 'sub'))
- attn_gain_grad: float32 [1536], P(('seq', 'sub'))
- query_gain_grad: float32 [1536], P(('seq', 'sub'))
- key_gain_grad: float32 [1536], P(('seq', 'sub'))
- text_key_gain_grad: float32 [1536], P(('seq', 'sub'))
- attn_out_gain_grad: float32 [1536], P(('seq', 'sub'))
- ffn_gain_grad: float32 [1536], P(('seq', 'sub'))
- ffn_out_gain_grad: float32 [1536], P(('seq', 'sub'))
- cross_gate_grad: float32 [24], replicated
The draws below stay inside these ranges and needn't reach their ends.
Inputs may be any that keep to these rules, and one draw needn't show every extreme that they name: `clip_lengths`: clip lengths sum to 4096; the longest clip has exactly 2048 tokens. `cap_lengths`: one clip's caption fills all 256 slots.
All inputs are finite; a program needn't handle non-finite values.
Results may differ from the reference program's by a relative error of at most 0.04.
Values may be sent and summed in bfloat16 or wider, within the bound.
No kernel may reach another device: no remote copies, remote signals or barrier semaphores. Data moves between devices by JAX's collectives and lax.ppermute only.
A program may use at most 384 MiB of HBM per device.

```python
import math
import jax
import jax.numpy as jnp
import numpy as np
from jax import lax

D = 1536
H = 24
HD = 64
FF = 4096
TD = 4096
COND = 1024
CLIPS = 5
CAP = 256
TOKENS = 4096
CAPTOK = 1280


def draw_cap_lengths(key, part):
    key_draw, key_pick = jax.random.split(jax.random.fold_in(key, 17))
    lengths_drawn = jax.random.randint(key_draw, (CLIPS,), CAP // 4, CAP + 1)
    chosen = jax.random.randint(key_pick, (), 0, CLIPS)
    return jnp.where(jnp.arange(CLIPS) == chosen, CAP, lengths_drawn).astype(jnp.int32)


def place_ends(entries, rng, least, largest):
    longest = entries.shape.index(max(entries.shape))
    spots = []
    for shift in (0, 1):
        where = [jax.random.randint(jax.random.fold_in(rng, axis), (), 0, length) for axis, length in enumerate(entries.shape)]
        where[longest] = (where[longest] + shift) % entries.shape[longest]
        spots.append(tuple(where))
    return entries.at[spots[0]].set(least).at[spots[1]].set(largest)


def levels(own_key, extent, cuts, smallest, high):
    loudness, own = 1.0, jax.random.fold_in(own_key, 6)
    for position, blocks in cuts:
        steps = jnp.exp(jax.random.uniform(jax.random.fold_in(own, position), (blocks,), jnp.float32, smallest / len(cuts), high / len(cuts)))
        loudness = loudness * jnp.repeat(steps, extent[position] // blocks).reshape([-1 if axis == position else 1 for axis in range(len(extent))])
    return loudness


def profile(number_of, total, reach, skew):
    weights = [(1 << 20) // math.isqrt(grade ** skew) + 1 for grade in range(2, number_of + 1)]
    surplus, counts = total - reach - (number_of - 1), [1] * (number_of - 1)
    while surplus > 0:
        movable = [i for i in range(number_of - 1) if counts[i] < reach]
        mass, remaining = sum([weights[i] for i in movable]), surplus
        for i in movable:
            more = min(reach - counts[i], max(1, remaining * weights[i] // mass), surplus)
            counts[i] = counts[i] + more
            surplus = surplus - more
    return np.array([reach] + counts)


def ragged(key, number_of, total, bound, lean):
    if number_of == 2:
        one = jax.random.randint(key, (), max(1, total - bound), min(bound, total - 1) + 1)
        return jnp.stack([one, total - one])
    sizes = jnp.asarray(profile(number_of, total, bound, lean), jnp.int32)
    twos = (number_of - 1) // 2
    source_of, taker = sizes[1:1 + 2 * twos:2], sizes[2:2 + 2 * twos:2]
    margin = jnp.minimum(source_of - 1, bound - taker)
    moved = jax.random.randint(jax.random.fold_in(key, 1), (twos,), 0, 1 << 20) % (margin + 1)
    sizes = sizes.at[1:1 + 2 * twos:2].set(source_of - moved).at[2:2 + 2 * twos:2].set(taker + moved)
    return sizes[jax.random.permutation(jax.random.fold_in(key, 2), number_of)]


def scatter_about(own_key, shape, scale, reach, cuts=(), kind=jnp.bfloat16):
    values = jax.random.normal(own_key, shape, jnp.float32) * scale
    if len(cuts) > 0:
        values = levels(own_key, shape, cuts, -0.22, 0.18) * values
    return jnp.clip(values, min=-reach, max=reach).astype(kind)


def setup_inputs(seed: int = 0) -> dict:
    keys = jax.random.split(jax.random.key(seed), 27)
    video = scatter_about(keys[0], (TOKENS, D), 1.0, 6.0, ((0, 32),))
    conditioning = scatter_about(keys[1], (CLIPS, COND), 1.0, 6.0)
    captions = scatter_about(keys[2], (CAPTOK, TD), 1.0, 6.0, ((0, 4),))
    clip_lengths = ragged(keys[3], CLIPS, TOKENS, TOKENS // 2, 2).astype(jnp.int32)
    cap_lengths = draw_cap_lengths(jax.random.fold_in(keys[26], 71), 0)
    positions = place_ends(jax.random.randint(keys[5], (TOKENS, 3), 0, 64), jax.random.fold_in(keys[5], 1), 0, 63).astype(jnp.int32)
    ada_weight = scatter_about(keys[6], (COND, 4 * D), COND ** -0.5, 0.1875, ((0, 32),))
    ada_bias = scatter_about(keys[7], (4 * D,), 0.5, 3.0, ((0, 32),))
    query_weight = scatter_about(keys[8], (D, D), D ** -0.5, 0.15625, ((0, 32),))
    key_weight = scatter_about(keys[9], (D, D), D ** -0.5, 0.15625, ((0, 32),))
    value_weight = scatter_about(keys[10], (D, D), D ** -0.5, 0.15625, ((0, 32),))
    out_weight = scatter_about(keys[11], (D, D), D ** -0.5, 0.15625, ((0, 32),))
    text_key_weight = scatter_about(keys[12], (TD, D), TD ** -0.5, 0.09375, ((0, 32),))
    text_value_weight = scatter_about(keys[13], (TD, D), TD ** -0.5, 0.09375, ((0, 32),))
    gate_weight = scatter_about(keys[14], (D, FF), D ** -0.5, 0.15625, ((0, 32),))
    up_weight = scatter_about(keys[15], (D, FF), D ** -0.5, 0.15625, ((0, 32),))
    down_weight = scatter_about(keys[16], (FF, D), FF ** -0.5, 0.09375, ((0, 32),))
    attn_gain = jnp.clip(1.0 + 0.1 * jax.random.normal(keys[17], (D,), jnp.float32), 0.5, 1.5).astype(jnp.bfloat16)
    query_gain = jnp.clip(1.0 + 0.1 * jax.random.normal(keys[18], (D,), jnp.float32), 0.5, 1.5).astype(jnp.bfloat16)
    key_gain = jnp.clip(1.0 + 0.1 * jax.random.normal(keys[19], (D,), jnp.float32), 0.5, 1.5).astype(jnp.bfloat16)
    text_key_gain = jnp.clip(1.0 + 0.1 * jax.random.normal(keys[20], (D,), jnp.float32), 0.5, 1.5).astype(jnp.bfloat16)
    attn_out_gain = jnp.clip(1.0 + 0.1 * jax.random.normal(keys[21], (D,), jnp.float32), 0.5, 1.5).astype(jnp.bfloat16)
    ffn_gain = jnp.clip(1.0 + 0.1 * jax.random.normal(keys[22], (D,), jnp.float32), 0.5, 1.5).astype(jnp.bfloat16)
    ffn_out_gain = jnp.clip(1.0 + 0.1 * jax.random.normal(keys[23], (D,), jnp.float32), 0.5, 1.5).astype(jnp.bfloat16)
    cross_gate = jnp.clip(jax.random.uniform(keys[24], (H,), jnp.float32, -1.5, 1.5), -1.5, 1.5).astype(jnp.bfloat16)
    cotangent = scatter_about(keys[25], (TOKENS, D), 1.0, 6.0, ((0, 32),))
    return {"video": video, "conditioning": conditioning, "captions": captions, "clip_lengths": clip_lengths, "cap_lengths": cap_lengths, "positions": positions, "ada_weight": ada_weight, "ada_bias": ada_bias, "query_weight": query_weight, "key_weight": key_weight, "value_weight": value_weight, "out_weight": out_weight, "text_key_weight": text_key_weight, "text_value_weight": text_value_weight, "gate_weight": gate_weight, "up_weight": up_weight, "down_weight": down_weight, "attn_gain": attn_gain, "query_gain": query_gain, "key_gain": key_gain, "text_key_gain": text_key_gain, "attn_out_gain": attn_out_gain, "ffn_gain": ffn_gain, "ffn_out_gain": ffn_out_gain, "cross_gate": cross_gate, "cotangent": cotangent}


epsilon = 1e-06
rope_base = 10000.0
masked_score = -1e+30
highest = lax.Precision.HIGHEST

@jax.custom_vjp
def low(v):
    return lax.optimization_barrier(v.astype(jnp.bfloat16)).astype(jnp.float32)

@jax.custom_vjp
def low_back(v):
    return v

def low_keep(v):
    return (low(v), None)

def low_pass(kept, grad):
    return (grad,)

def back_keep(v):
    return (v, None)

def back_low(kept, grad):
    return (low(grad),)
low.defvjp(low_keep, low_pass)
low_back.defvjp(back_keep, back_low)

def rms_norm(values):
    return values * lax.rsqrt(lax.optimization_barrier(jnp.mean(values * values, -1, keepdims=True)) + epsilon)

def rope_tables(positions, head_dim):
    pair_total = head_dim // 2
    frame_pairs = pair_total // 4
    height_pairs = (pair_total - frame_pairs) // 2
    width_pairs = pair_total - frame_pairs - height_pairs
    pieces = []
    for axis_id, pair_count in enumerate((frame_pairs, height_pairs, width_pairs)):
        frequency = rope_base ** (-jnp.arange(pair_count, dtype=jnp.float32) / pair_count)
        pieces.append(positions[:, axis_id].astype(jnp.float32)[:, None] * frequency[None, :])
    angles = jnp.concatenate(pieces, 1)
    return (jnp.cos(angles), jnp.sin(angles))

def rotate(values, cosine, sine):
    shaped = values.reshape(values.shape[0], values.shape[1], -1, 2)
    even_part = shaped[..., 0]
    odd_part = shaped[..., 1]
    cos_part = cosine[:, None, :]
    sin_part = sine[:, None, :]
    turned = jnp.stack([even_part * cos_part - odd_part * sin_part, even_part * sin_part + odd_part * cos_part], -1)
    return turned.reshape(values.shape)

def clip_index(token_index, clip_lengths):
    bounds = jnp.cumsum(clip_lengths)
    return lax.optimization_barrier(jnp.sum((token_index[:, None] >= bounds[None, :]).astype(jnp.int32), 1))

def attend(queries, key_rows, values, query_clip, key_clip, key_valid):
    rows_total = queries.shape[0]
    block_rows = min(256, rows_total)
    query_blocks = queries.reshape(rows_total // block_rows, block_rows, queries.shape[1], queries.shape[2])
    clip_blocks = query_clip.reshape(rows_total // block_rows, block_rows)

    def one_block(inputs):
        query_blk, clip_blk = inputs
        scores = low_back(jnp.einsum('qhd,khd->qhk', query_blk, key_rows, precision=highest) / math.sqrt(queries.shape[2]))
        allowed = ((clip_blk[:, None] == key_clip[None, :]) & key_valid[None, :])[:, None, :]
        weights = low(jax.nn.softmax(jnp.where(allowed, scores, masked_score), -1))
        return jnp.einsum('qhk,khd->qhd', weights, values, precision=highest)
    result = lax.map(jax.checkpoint(one_block), (query_blocks, clip_blocks))
    return result.reshape(queries.shape)

def reference(video, conditioning, captions, clip_lengths, cap_lengths, positions, ada_weight, ada_bias, query_weight, key_weight, value_weight, out_weight, text_key_weight, text_value_weight, gate_weight, up_weight, down_weight, attn_gain, query_gain, key_gain, text_key_gain, attn_out_gain, ffn_gain, ffn_out_gain, cross_gate, cotangent):
    token_clip = clip_index(jnp.arange(TOKENS, dtype=jnp.int32), clip_lengths)
    cap_row = jnp.arange(CAPTOK, dtype=jnp.int32)
    caption_clip = cap_row // CAP
    caption_valid = cap_row % CAP < cap_lengths[caption_clip]
    all_valid = jnp.ones((TOKENS,), jnp.bool_)
    cosine, sine = rope_tables(positions, HD)

    def forward(video_in, cond_in, caption_in, ada_w, ada_b, query_w, key_w, value_w, out_w, text_key_w, text_value_w, gate_w, up_w, down_w, attn_g, query_g, key_g, text_key_g, attn_out_g, ffn_g, ffn_out_g, gate_h):
        modulation = low_back(jnp.dot(low(jax.nn.silu(cond_in)), ada_w, precision=highest) + ada_b)
        per_token = modulation[token_clip]
        attn_scale = per_token[:, :D]
        attn_gate = per_token[:, D:2 * D]
        ffn_scale = per_token[:, 2 * D:3 * D]
        ffn_gate = per_token[:, 3 * D:]
        normed = low(rms_norm(video_in) * attn_g * (1.0 + attn_scale))
        query_pre = low_back(jnp.dot(normed, query_w, precision=highest))
        key_pre = low_back(jnp.dot(normed, key_w, precision=highest))
        values = low_back(low(jnp.dot(normed, value_w, precision=highest))).reshape(TOKENS, H, HD)
        queries = low_back(low(rotate((rms_norm(query_pre) * query_g).reshape(TOKENS, H, HD), cosine, sine)))
        key_rows = low_back(low(rotate((rms_norm(key_pre) * key_g).reshape(TOKENS, H, HD), cosine, sine)))
        text_key_pre = low_back(jnp.dot(caption_in, text_key_w, precision=highest))
        text_keys = low_back(low(rms_norm(text_key_pre) * text_key_g)).reshape(CAPTOK, H, HD)
        text_values = low_back(low(jnp.dot(caption_in, text_value_w, precision=highest))).reshape(CAPTOK, H, HD)
        self_out = low(attend(queries, key_rows, values, token_clip, token_clip, all_valid))
        cross_out = low_back(attend(queries, text_keys, text_values, token_clip, caption_clip, caption_valid))
        mixed = low_back(low((self_out + jnp.tanh(gate_h)[None, :, None] * cross_out).reshape(TOKENS, D)))
        projected = low_back(jnp.dot(mixed, out_w, precision=highest))
        hidden_state = video_in + jnp.tanh(attn_gate) * rms_norm(projected) * attn_out_g
        ffn_in = low(rms_norm(hidden_state) * ffn_g * (1.0 + ffn_scale))
        gate_pre = low_back(jnp.dot(ffn_in, gate_w, precision=highest))
        up_pre = low_back(jnp.dot(ffn_in, up_w, precision=highest))
        activated = low(jax.nn.silu(gate_pre) * up_pre)
        down_out = low_back(jnp.dot(activated, down_w, precision=highest))
        return hidden_state + jnp.tanh(ffn_gate) * rms_norm(down_out) * ffn_out_g
    params = tuple((array_in.astype(jnp.float32) for array_in in (video, conditioning, captions, ada_weight, ada_bias, query_weight, key_weight, value_weight, out_weight, text_key_weight, text_value_weight, gate_weight, up_weight, down_weight, attn_gain, query_gain, key_gain, text_key_gain, attn_out_gain, ffn_gain, ffn_out_gain, cross_gate)))
    result, pullback = jax.vjp(forward, *params)
    gradients = pullback(cotangent.astype(jnp.float32))
    return (result.astype(jnp.bfloat16), gradients[0], gradients[2], gradients[1], gradients[3], gradients[4], gradients[5], gradients[6], gradients[7], gradients[8], gradients[9], gradients[10], gradients[11], gradients[12], gradients[13], gradients[14], gradients[15], gradients[16], gradients[17], gradients[18], gradients[19], gradients[20], gradients[21])
```

```python
import functools
import math

import jax
import jax.numpy as jnp
from jax import lax
from jax.experimental import pallas as pl
from jax.experimental.pallas import tpu as pltpu
from jax.sharding import PartitionSpec as P

CAP = 256
LANES = 128
BLOCK = 256

epsilon = 1e-06
rope_base = 10000.0
masked_score = -1e30
highest = lax.Precision.HIGHEST
f32 = jnp.float32
bf16 = jnp.bfloat16
NT = (((1,), (1,)), ((), ()))
TN = (((0,), (0,)), ((), ()))
NN = (((1,), (0,)), ((), ()))
BOTH = ("seq", "sub")


def dot(a, b, dims=NN):
    return lax.dot_general(a, b, dims, preferred_element_type=f32)


def inv_rms(values):
    return lax.rsqrt(jnp.mean(values * values, -1, keepdims=True) + epsilon)


def norm_back(normed_hat, inverse, grad_hat):
    return inverse * (grad_hat - normed_hat * jnp.mean(normed_hat * grad_hat, -1, keepdims=True))


def round_keep(values):
    return lax.optimization_barrier(values.astype(bf16)).astype(f32)


def shift_pairs(count, step):
    return [(i, (i + step) % count) for i in range(count)]


def gather_sub(x):
    count = lax.axis_size("sub")
    me = lax.axis_index("sub")
    rows = x.shape[0]
    rest = (0,) * (x.ndim - 1)
    out = lax.dynamic_update_slice(
        jnp.zeros((count * rows,) + x.shape[1:], x.dtype), x, (me * rows,) + rest
    )
    for step in range(1, count):
        got = lax.ppermute(x, "sub", shift_pairs(count, step))
        out = lax.dynamic_update_slice(out, got, ((me - step) % count * rows,) + rest)
    return out


def exchange_sub(x):
    count = lax.axis_size("sub")
    me = lax.axis_index("sub")
    out = x
    for step in range(1, count):
        block = lax.dynamic_slice_in_dim(x, (me + step) % count, 1, 0)
        got = lax.ppermute(block, "sub", shift_pairs(count, step))
        out = lax.dynamic_update_slice_in_dim(out, got, (me - step) % count, 0)
    return out


def scatter_sub(x):
    count = lax.axis_size("sub")
    me = lax.axis_index("sub")
    rows = x.shape[0] // count
    total = lax.dynamic_slice_in_dim(x, me * rows, rows, 0)
    low = x.astype(bf16)
    for step in range(1, count):
        block = lax.dynamic_slice_in_dim(low, (me + step) % count * rows, rows, 0)
        got = lax.ppermute(block, "sub", shift_pairs(count, step))
        total = total + got.astype(f32)
    return total


def pad_lanes(x):
    extra = -x.shape[-1] % LANES
    if extra == 0:
        return x
    return jnp.pad(x, [(0, 0)] * (x.ndim - 1) + [(0, extra)])


def attn_fwd_kernel(scale, rng_ref, lo_ref, hi_ref, q_ref, k_ref, v_ref, o_ref, lse_ref):
    rows = q_ref.shape[0]
    half = LANES // 2
    lane = lax.broadcasted_iota(jnp.int32, (BLOCK, LANES), 1)
    for qb in range(rows // BLOCK):
        cut = slice(qb * BLOCK, (qb + 1) * BLOCK)
        q = q_ref[cut, :]
        zero = jnp.zeros_like(q)
        qs = (jnp.where(lane < half, q, zero), jnp.where(lane >= half, q, zero))
        lo = lo_ref[0:1, cut]
        hi = hi_ref[0:1, cut]

        def step(i, carry):
            stats, acc = carry
            at = pl.ds(pl.multiple_of(i * BLOCK, BLOCK), BLOCK)
            k = k_ref[at, :]
            v = v_ref[at, :]
            index = i * BLOCK + lax.broadcasted_iota(jnp.int32, (BLOCK, BLOCK), 0)
            allowed = (index >= lo) & (index < hi)
            new_stats = []
            parts = []
            for h in range(2):
                top, norm = stats[h]
                scores = jnp.where(allowed, dot(k, qs[h], NT) * scale, masked_score)
                new_top = jnp.maximum(top, jnp.max(scores, 0, keepdims=True))
                probs = jnp.exp(scores - new_top)
                factor = jnp.exp(top - new_top)
                norm = norm * factor + jnp.sum(probs, 0, keepdims=True)
                out = dot(v, probs.astype(bf16), TN)[h * half : (h + 1) * half, :]
                parts.append(acc[h * half : (h + 1) * half, :] * factor + out)
                new_stats.append((new_top, norm))
            return tuple(new_stats), jnp.concatenate(parts, 0)

        first = (jnp.full((1, BLOCK), masked_score, f32), jnp.zeros((1, BLOCK), f32))
        stats, acc = lax.fori_loop(
            rng_ref[qb, 0],
            rng_ref[qb, 1],
            step,
            ((first, first), jnp.zeros((LANES, BLOCK), f32)),
        )
        for h in range(2):
            top, norm = stats[h]
            o_ref[h * half : (h + 1) * half, cut] = acc[h * half : (h + 1) * half, :] / norm
            lse_ref[h : h + 1, cut] = top + jnp.log(norm)


def attn_bwd_kernel(
    scale, rng_ref, lo_ref, hi_ref, q_ref, k_ref, v_ref, g_ref, o_ref, lse_ref, dq_ref, dkv_ref, dk, dv
):
    rows = q_ref.shape[0]
    half = LANES // 2
    lane = lax.broadcasted_iota(jnp.int32, (BLOCK, LANES), 1)
    keys = k_ref.shape[0]

    def clear(i, unused):
        at = pl.ds(pl.multiple_of(i * BLOCK, BLOCK), BLOCK)
        dk[at, :] = jnp.zeros((BLOCK, LANES), f32)
        dv[at, :] = jnp.zeros((BLOCK, LANES), f32)
        return unused

    lax.fori_loop(0, keys // BLOCK, clear, 0)
    for qb in range(rows // BLOCK):
        cut = slice(qb * BLOCK, (qb + 1) * BLOCK)
        q = q_ref[cut, :]
        g = g_ref[cut, :]
        zero = jnp.zeros_like(q)
        qs = (jnp.where(lane < half, q, zero), jnp.where(lane >= half, q, zero))
        gs = (jnp.where(lane < half, g, zero), jnp.where(lane >= half, g, zero))
        product = jnp.transpose(g.astype(f32)) * o_ref[:, cut]
        deltas = [
            jnp.sum(product[h * half : (h + 1) * half, :], 0, keepdims=True) for h in range(2)
        ]
        logs = [lse_ref[h : h + 1, cut] for h in range(2)]
        lo = lo_ref[0:1, cut]
        hi = hi_ref[0:1, cut]

        def step(i, dq):
            at = pl.ds(pl.multiple_of(i * BLOCK, BLOCK), BLOCK)
            k = k_ref[at, :]
            v = v_ref[at, :]
            index = i * BLOCK + lax.broadcasted_iota(jnp.int32, (BLOCK, BLOCK), 0)
            allowed = (index >= lo) & (index < hi)
            dk_new = dk[at, :]
            dv_new = dv[at, :]
            terms = []
            for h in range(2):
                scores = dot(k, qs[h], NT) * scale
                probs = jnp.where(allowed, jnp.exp(scores - logs[h]), 0.0)
                prob_grad = dot(v, gs[h], NT)
                score_grad = (probs * (prob_grad - deltas[h])).astype(bf16)
                dv_new = dv_new + dot(probs.astype(bf16), gs[h])
                dk_new = dk_new + dot(score_grad, qs[h])
                terms.append(dot(score_grad, k, TN))
            dk[at, :] = dk_new
            dv[at, :] = dv_new
            return dq + jnp.where(lane < half, terms[0], terms[1])

        dq = lax.fori_loop(
            rng_ref[qb, 0], rng_ref[qb, 1], step, jnp.zeros((BLOCK, LANES), f32)
        )
        dq_ref[cut, :] = dq * scale

    def flush(i, unused):
        at = pl.ds(pl.multiple_of(i * BLOCK, BLOCK), BLOCK)
        dkv_ref[at, 0:LANES] = (dk[at, :] * scale).astype(bf16)
        dkv_ref[at, LANES : 2 * LANES] = dv[at, :].astype(bf16)
        return unused

    lax.fori_loop(0, keys // BLOCK, flush, 0)


def column(rows, width=LANES, shift=0):
    return pl.BlockSpec((rows, width), lambda p: (0, p + shift))


def whole(array):
    return pl.BlockSpec(array.shape, lambda p: (0, 0))


def attn_forward(name, scale, spans, q, kv):
    lo, hi, rng = spans
    rows, width = q.shape
    keys = kv.shape[0]
    pairs = width // LANES
    return pl.pallas_call(
        functools.partial(attn_fwd_kernel, scale),
        grid=(pairs,),
        in_specs=[
            pl.BlockSpec(memory_space=pltpu.SMEM),
            whole(lo),
            whole(hi),
            column(rows),
            column(keys),
            column(keys, shift=pairs),
        ],
        out_specs=[
            pl.BlockSpec((LANES, rows), lambda p: (p, 0)),
            pl.BlockSpec((8, rows), lambda p: (p, 0)),
        ],
        out_shape=[
            jax.ShapeDtypeStruct((width, rows), f32),
            jax.ShapeDtypeStruct((pairs * 8, rows), f32),
        ],
        compiler_params=pltpu.CompilerParams(vmem_limit_bytes=56 * 1024 * 1024),
        cost_estimate=pl.CostEstimate(
            flops=4 * rows * keys * width // 2,
            bytes_accessed=4 * keys * width,
            transcendentals=rows * keys * width // 128,
        ),
        name=name,
    )(rng, lo, hi, q, kv, kv)


def attn_backward(name, scale, spans, q, kv, grad, out, lse):
    lo, hi, rng = spans
    rows, width = q.shape
    keys = kv.shape[0]
    pairs = width // LANES
    return pl.pallas_call(
        functools.partial(attn_bwd_kernel, scale),
        grid=(pairs,),
        in_specs=[
            pl.BlockSpec(memory_space=pltpu.SMEM),
            whole(lo),
            whole(hi),
            column(rows),
            column(keys),
            column(keys, shift=pairs),
            column(rows),
            pl.BlockSpec((LANES, rows), lambda p: (p, 0)),
            pl.BlockSpec((8, rows), lambda p: (p, 0)),
        ],
        out_specs=[column(rows), column(keys, 2 * LANES)],
        out_shape=[
            jax.ShapeDtypeStruct((rows, width), f32),
            jax.ShapeDtypeStruct((keys, 2 * width), bf16),
        ],
        scratch_shapes=[pltpu.VMEM((keys, LANES), f32), pltpu.VMEM((keys, LANES), f32)],
        compiler_params=pltpu.CompilerParams(vmem_limit_bytes=56 * 1024 * 1024),
        cost_estimate=pl.CostEstimate(
            flops=10 * rows * keys * width // 2,
            bytes_accessed=8 * keys * width,
            transcendentals=rows * keys * width // 128,
        ),
        name=name,
    )(rng, lo, hi, q, kv, kv, grad, out, lse)


def split_pairs(x, width):
    rows = x.shape[0]
    shaped = x.reshape(rows, -1, 2, LANES)
    return (
        shaped[:, :, 0].reshape(rows, -1)[:, :width],
        shaped[:, :, 1].reshape(rows, -1)[:, :width],
    )


def make_spans(lo, hi):
    first = lo[::BLOCK] // BLOCK
    last = (hi[BLOCK - 1 :: BLOCK] + BLOCK - 1) // BLOCK
    return lo[None, :], hi[None, :], jnp.stack([first, last], 1)


def rope_tables(positions, head_dim, width):
    pair_total = head_dim // 2
    frame_pairs = pair_total // 4
    height_pairs = (pair_total - frame_pairs) // 2
    width_pairs = pair_total - frame_pairs - height_pairs
    pieces = []
    for axis_id, pair_count in enumerate((frame_pairs, height_pairs, width_pairs)):
        frequency = rope_base ** (-jnp.arange(pair_count, dtype=f32) / pair_count)
        row = [jnp.zeros((n,), f32) for n in (frame_pairs, height_pairs, width_pairs)]
        row[axis_id] = frequency
        pieces.append(jnp.tile(jnp.repeat(jnp.concatenate(row), 2), LANES // head_dim))
    where = positions.astype(f32)
    angles = sum(where[:, i : i + 1] * pieces[i][None, :] for i in range(3))
    odd = lax.broadcasted_iota(jnp.int32, angles.shape, 1) % 2 == 1
    cosine = jnp.cos(angles)
    sine = jnp.sin(angles)
    sine = jnp.where(odd, sine, -sine)
    copies = -(-width // LANES)
    return (
        jnp.concatenate([cosine] * copies, 1)[:, :width],
        jnp.concatenate([sine] * copies, 1)[:, :width],
    )


def swap_pairs(x):
    odd = lax.broadcasted_iota(jnp.int32, x.shape, 1) % 2 == 1
    return jnp.where(odd, jnp.roll(x, 1, 1), jnp.roll(x, -1, 1))


def clip_index(token_index, clip_lengths):
    bounds = jnp.cumsum(clip_lengths)
    return jnp.sum((token_index[:, None] >= bounds[None, :]).astype(jnp.int32), 1)


def embed(value, size, start, axis=-1):
    axis = axis % value.ndim
    shape = list(value.shape)
    shape[axis] = size
    return lax.dynamic_update_slice_in_dim(jnp.zeros(shape, value.dtype), value, start, axis)


def body(
    video,
    conditioning,
    captions,
    clip_lengths,
    cap_lengths,
    positions,
    ada_weight,
    ada_bias,
    query_weight,
    key_weight,
    value_weight,
    out_weight,
    text_key_weight,
    text_value_weight,
    gate_weight,
    up_weight,
    down_weight,
    attn_gain,
    query_gain,
    key_gain,
    text_key_gain,
    attn_out_gain,
    ffn_gain,
    ffn_out_gain,
    cross_gate,
    cotangent,
):
    num_sub = lax.axis_size("sub")
    num_seq = lax.axis_size("seq")
    tok_rows, model_width = video.shape
    heads_total = cross_gate.shape[0]
    head_dim = model_width // heads_total
    heads_local = heads_total // num_sub
    local_width = heads_local * head_dim
    score_scale = 1.0 / math.sqrt(head_dim)
    sub_index = lax.axis_index("sub")
    seq_index = lax.axis_index("seq")
    device_index = seq_index * num_sub + sub_index
    group_rows = tok_rows * num_sub
    clip_count = clip_lengths.shape[0]
    clip_range = jnp.arange(clip_count, dtype=jnp.int32)
    rows = query_weight.shape[0]
    text_rows = text_key_weight.shape[0]
    hidden_rows = down_weight.shape[0]
    hidden_local = num_seq * hidden_rows
    lanes = local_width + (-local_width % LANES)

    video_group = gather_sub(video)
    positions_group = gather_sub(positions)

    def by_sub(weight):
        return weight.reshape(weight.shape[0], num_sub, -1)

    qkv_shard = jnp.concatenate([by_sub(w) for w in (query_weight, key_weight, value_weight)], 2)
    qkv_full = lax.all_gather(
        exchange_sub(qkv_shard.transpose(1, 0, 2)).reshape(num_sub * rows, 3 * local_width),
        "seq", axis=0, tiled=True,
    )
    text_shard = jnp.concatenate([by_sub(w) for w in (text_key_weight, text_value_weight)], 2)
    text_full = lax.all_gather(
        exchange_sub(text_shard.transpose(1, 0, 2)).reshape(num_sub * text_rows, 2 * local_width),
        "seq", axis=0, tiled=True,
    )

    def hidden_by_sub(weight):
        shaped = weight.reshape(rows, num_seq, num_sub, hidden_rows).transpose(2, 0, 1, 3)
        return shaped.reshape(num_sub, rows, hidden_local)

    ffn_shard = jnp.concatenate([hidden_by_sub(gate_weight), hidden_by_sub(up_weight)], 2)
    out_move = [
        (j, j % num_seq * num_sub + j // num_seq) for j in range(num_seq * num_sub)
    ]
    out_full = lax.all_gather(
        lax.ppermute(out_weight, BOTH, out_move), "seq", axis=0, tiled=True
    )
    ffn_full = lax.all_gather(
        exchange_sub(ffn_shard).reshape(num_sub * rows, 2 * hidden_local),
        "seq", axis=0, tiled=True,
    )
    down_full = lax.all_gather(down_weight, "seq", axis=0, tiled=True)

    cond_float = conditioning.astype(f32)
    cond_act = jax.nn.silu(cond_float).astype(bf16)
    cond_rows, mod_width = ada_weight.shape
    cond_slice = lax.dynamic_slice_in_dim(cond_act, device_index * cond_rows, cond_rows, 1)
    bias_rows = ada_bias.shape[0]
    mod_part = dot(cond_slice, ada_weight) + embed(
        ada_bias.astype(f32)[None], mod_width, device_index * bias_rows
    )
    gain_shard = jnp.stack(
        [attn_gain, query_gain, key_gain, text_key_gain, attn_out_gain, ffn_gain, ffn_out_gain]
    ).astype(f32)
    modulation, gains = lax.psum(
        (mod_part, embed(gain_shard, model_width, device_index * rows)), BOTH
    )
    attn_gain_f = gains[0]
    attn_out_f = gains[4]
    ffn_gain_f = gains[5]
    ffn_out_f = gains[6]

    def own_columns(value):
        return lax.dynamic_slice_in_dim(value, sub_index * local_width, local_width, 0)

    query_gain_f = own_columns(gains[1])
    key_gain_f = own_columns(gains[2])
    text_key_gain_f = own_columns(gains[3])

    token_index = device_index * tok_rows + jnp.arange(tok_rows, dtype=jnp.int32)
    token_clip = clip_index(token_index, clip_lengths)
    clip_onehot = (token_clip[:, None] == clip_range[None, :]).astype(f32)
    per_token = jnp.dot(clip_onehot, modulation, precision=highest)
    attn_scale = per_token[:, :model_width]
    attn_gate = per_token[:, model_width : 2 * model_width]
    ffn_scale = per_token[:, 2 * model_width : 3 * model_width]
    ffn_gate = per_token[:, 3 * model_width :]

    group_index = seq_index * group_rows + jnp.arange(group_rows, dtype=jnp.int32)
    group_clip = clip_index(group_index, clip_lengths)
    group_hot = group_clip[:, None] == clip_range[None, :]

    def of_clip(values):
        return jnp.sum(jnp.where(group_hot, values[None, :], 0), 1)

    clip_ends = jnp.cumsum(clip_lengths)
    self_spans = make_spans(of_clip(clip_ends - clip_lengths), of_clip(clip_ends))
    cross_spans = make_spans(group_clip * CAP, group_clip * CAP + of_clip(cap_lengths))

    group_scale = jnp.dot(group_hot.astype(f32), modulation[:, :model_width], precision=highest)
    video_g = video_group.astype(f32)
    normed = (video_g * inv_rms(video_g) * (attn_gain_f * (1.0 + group_scale))).astype(bf16)
    qkv_pre = dot(normed, qkv_full)
    query_pre = qkv_pre[:, :local_width]
    key_pre = qkv_pre[:, local_width : 2 * local_width]
    values_own = qkv_pre[:, 2 * local_width :].astype(bf16)

    cap_shard = captions.shape[0]
    cap_rows = cap_shard // num_seq
    cap_group = gather_sub(lax.dynamic_slice_in_dim(captions, seq_index * cap_rows, cap_rows, 0))
    text_pre = dot(cap_group, text_full)
    text_key_pre = text_pre[:, :local_width]

    def sum_sub(*parts):
        return lax.psum(jnp.stack(parts), "sub")

    text_square = sum_sub(jnp.sum(text_key_pre * text_key_pre, 1))
    text_inv = lax.rsqrt(text_square[0] / model_width + epsilon)[:, None]
    text_hat = text_key_pre * text_inv
    text_keys = (text_hat * text_key_gain_f).astype(bf16)
    text_values = text_pre[:, local_width:].astype(bf16)
    text_kv = lax.all_gather(
        jnp.concatenate([pad_lanes(text_keys), pad_lanes(text_values)], 1), "seq", axis=0, tiled=True
    )
    text_kv = text_kv.reshape(num_seq, num_sub, cap_rows, 2 * lanes).transpose(1, 0, 2, 3)
    text_kv = text_kv.reshape(num_sub * cap_shard, 2 * lanes)

    squares = sum_sub(jnp.sum(query_pre * query_pre, 1), jnp.sum(key_pre * key_pre, 1))
    inverses = lax.rsqrt(squares / model_width + epsilon)
    query_inv = inverses[0][:, None]
    key_inv = inverses[1][:, None]
    query_hat = query_pre * query_inv
    key_hat = key_pre * key_inv
    cosine, sine = rope_tables(positions_group, head_dim, local_width)

    def turn(value):
        return value * cosine + swap_pairs(value) * sine

    def turn_back(value):
        return value * cosine - swap_pairs(value) * sine

    queries = pad_lanes(turn(query_hat * query_gain_f).astype(bf16))
    keys_own = turn(key_hat * key_gain_f).astype(bf16)
    kv_all = lax.all_gather(
        jnp.concatenate([pad_lanes(keys_own), pad_lanes(values_own)], 1), "seq", axis=0, tiled=True
    )

    cross_t, cross_lse = attn_forward("cross_fwd", score_scale, cross_spans, queries, text_kv)
    self_t, self_lse = attn_forward("self_fwd", score_scale, self_spans, queries, kv_all)

    gate_tanh = jnp.tanh(cross_gate.astype(f32))
    own_gate = lax.dynamic_slice_in_dim(gate_tanh, sub_index * heads_local, heads_local, 0)
    gate_rows = jnp.repeat(own_gate, head_dim)
    mixed = (
        (
            self_t[:local_width].astype(bf16).astype(f32)
            + gate_rows[:, None] * cross_t[:local_width]
        )
        .astype(bf16)
        .T
    )
    projected = scatter_sub(dot(mixed, out_full))
    proj_inv = inv_rms(projected)
    proj_hat = projected * proj_inv
    attn_tanh = jnp.tanh(attn_gate)
    video_float = video.astype(f32)
    hidden_state = video_float + attn_tanh * proj_hat * attn_out_f
    hidden_inv = inv_rms(hidden_state)
    hidden_hat = hidden_state * hidden_inv
    ffn_mult = ffn_gain_f * (1.0 + ffn_scale)
    ffn_in = gather_sub((hidden_hat * ffn_mult).astype(bf16))
    ffn_pre = dot(ffn_in, ffn_full)
    gate_pre = ffn_pre[:, :hidden_local]
    up_pre = ffn_pre[:, hidden_local:]
    activated = (jax.nn.silu(gate_pre) * up_pre).astype(bf16)
    down_out = scatter_sub(dot(activated, down_full))
    down_inv = inv_rms(down_out)
    down_hat = down_out * down_inv
    ffn_tanh = jnp.tanh(ffn_gate)
    block_out = (hidden_state + ffn_tanh * down_hat * ffn_out_f).astype(bf16)

    grad_out = cotangent.astype(f32)
    down_grad = gather_sub(
        norm_back(down_hat, down_inv, grad_out * ffn_tanh * ffn_out_f).astype(bf16)
    )
    act_grad = dot(down_grad, down_full, NT)
    gate_sig = jax.nn.sigmoid(gate_pre)
    gate_grad = act_grad * up_pre * gate_sig * (1.0 + gate_pre * (1.0 - gate_sig))
    up_grad = act_grad * jax.nn.silu(gate_pre)
    ffn_grad = jnp.concatenate([gate_grad.astype(bf16), up_grad.astype(bf16)], 1)
    ffn_in_grad = scatter_sub(dot(ffn_grad, ffn_full, NT))
    hidden_grad = grad_out + norm_back(hidden_hat, hidden_inv, ffn_in_grad * ffn_mult)
    proj_grad = gather_sub(
        norm_back(proj_hat, proj_inv, hidden_grad * attn_tanh * attn_out_f).astype(bf16)
    )
    mixed_grad = dot(proj_grad, out_full, NT).astype(bf16)

    def reduce_seq(term):
        return lax.psum_scatter(term.astype(bf16), "seq", scatter_dimension=0, tiled=True)

    down_weight_grad = reduce_seq(dot(activated, down_grad, TN)).astype(f32)
    ffn_weight_sum = reduce_seq(dot(ffn_in, ffn_grad, TN))
    out_weight_sum = reduce_seq(dot(mixed, proj_grad, TN))

    mixed_grad_f = mixed_grad.astype(f32)
    gate_terms = jnp.sum(mixed_grad_f.T * cross_t[:local_width], 1)
    cross_gate_part = jnp.sum(gate_terms.reshape(heads_local, head_dim), 1) * (
        1.0 - own_gate * own_gate
    )
    cross_out_grad = (mixed_grad_f * gate_rows).astype(bf16)
    query_cross, text_terms = attn_backward(
        "cross_bwd", score_scale, cross_spans, queries, text_kv, pad_lanes(cross_out_grad), cross_t, cross_lse
    )
    text_terms = text_terms.reshape(num_sub, num_seq, cap_rows, -1).transpose(1, 0, 2, 3)
    text_sum = reduce_seq(text_terms.reshape(num_sub * cap_shard, -1))
    query_self, kv_terms = attn_backward(
        "self_bwd", score_scale, self_spans, queries, kv_all, pad_lanes(mixed_grad), self_t, self_lse
    )
    key_grad, value_grad = split_pairs(reduce_seq(kv_terms), local_width)

    text_key_low, text_value_low = split_pairs(text_sum, local_width)
    text_key_low = text_key_low.astype(f32)
    text_key_gain_part = jnp.sum(text_key_low * text_hat, 0)
    text_grad_hat = text_key_low * text_key_gain_f
    text_mean = sum_sub(jnp.sum(text_hat * text_grad_hat, 1))[0][:, None] / model_width
    text_key_pre_grad = text_inv * (text_grad_hat - text_hat * text_mean)
    text_grad = jnp.concatenate([text_key_pre_grad.astype(bf16), text_value_low], 1)
    text_weight_sum = reduce_seq(dot(cap_group, text_grad, TN))
    caption_rows_grad = scatter_sub(dot(text_grad, text_full, NT))
    caption_grad = lax.all_gather(
        caption_rows_grad.astype(bf16), "seq", axis=0, tiled=True
    ).astype(f32)

    query_norm_grad = turn_back(round_keep((query_self + query_cross)[:, :local_width]))
    key_norm_grad = turn_back(key_grad.astype(f32))
    query_gain_part = jnp.sum(query_norm_grad * query_hat, 0)
    key_gain_part = jnp.sum(key_norm_grad * key_hat, 0)
    query_grad_hat = query_norm_grad * query_gain_f
    key_grad_hat = key_norm_grad * key_gain_f
    means = sum_sub(
        jnp.sum(query_hat * query_grad_hat, 1), jnp.sum(key_hat * key_grad_hat, 1)
    ) / model_width
    query_pre_grad = query_inv * (query_grad_hat - query_hat * means[0][:, None])
    key_pre_grad = key_inv * (key_grad_hat - key_hat * means[1][:, None])
    qkv_grad = jnp.concatenate(
        [query_pre_grad.astype(bf16), key_pre_grad.astype(bf16), value_grad], 1
    )
    normed_grad = scatter_sub(dot(qkv_grad, qkv_full, NT))
    qkv_weight_sum = reduce_seq(dot(normed, qkv_grad, TN))

    video_inv = inv_rms(video_float)
    video_hat = video_float * video_inv
    attn_mult = attn_gain_f * (1.0 + attn_scale)
    video_grad = hidden_grad + norm_back(video_hat, video_inv, normed_grad * attn_mult)

    token_mod_grad = jnp.concatenate(
        [
            normed_grad * video_hat * attn_gain_f,
            hidden_grad * proj_hat * attn_out_f * (1.0 - attn_tanh * attn_tanh),
            ffn_in_grad * hidden_hat * ffn_gain_f,
            grad_out * down_hat * ffn_out_f * (1.0 - ffn_tanh * ffn_tanh),
        ],
        1,
    )
    mod_grad_part = jnp.einsum("tc,tm->cm", clip_onehot, token_mod_grad, precision=highest)
    own_parts = embed(
        jnp.stack([query_gain_part, key_gain_part, text_key_gain_part]),
        model_width,
        sub_index * local_width,
    )
    gain_part = jnp.concatenate(
        [
            jnp.stack(
                [
                    jnp.sum(normed_grad * video_hat * (1.0 + attn_scale), 0),
                    jnp.sum(hidden_grad * attn_tanh * proj_hat, 0),
                    jnp.sum(ffn_in_grad * hidden_hat * (1.0 + ffn_scale), 0),
                    jnp.sum(grad_out * ffn_tanh * down_hat, 0),
                ]
            ),
            own_parts,
        ],
        0,
    )
    mod_sum, gain_sum, gate_sum = lax.psum(
        (mod_grad_part, gain_part, embed(cross_gate_part, heads_total, sub_index * heads_local)),
        BOTH,
    )
    own_gains = lax.dynamic_slice_in_dim(gain_sum, device_index * rows, rows, 1)
    mod_low = mod_sum.astype(bf16)
    ada_bias_grad = jnp.sum(
        lax.dynamic_slice_in_dim(mod_low.astype(f32), device_index * bias_rows, bias_rows, 1), 0
    )
    ada_weight_grad = dot(cond_slice, mod_low, TN)
    cond_sig = jax.nn.sigmoid(cond_float)
    cond_part = embed(
        dot(mod_low, ada_weight, NT), conditioning.shape[1], device_index * cond_rows
    )
    cond_grad = (
        lax.psum(lax.psum(cond_part, "sub"), "seq")
        * cond_sig
        * (1.0 + cond_float * (1.0 - cond_sig))
    )

    def from_sub(term, count):
        shaped = exchange_sub(term.reshape(num_sub, -1, term.shape[1])).astype(f32)
        width = term.shape[1] // count
        return [shaped[:, :, i * width : (i + 1) * width] for i in range(count)]

    def join_columns(blocks):
        return blocks.transpose(1, 0, 2).reshape(blocks.shape[1], -1)

    def join_hidden(blocks):
        shaped = blocks.reshape(num_sub, rows, num_seq, hidden_rows).transpose(1, 2, 0, 3)
        return shaped.reshape(rows, -1)

    query_weight_grad, key_weight_grad, value_weight_grad = (
        join_columns(b) for b in from_sub(qkv_weight_sum, 3)
    )
    text_key_weight_grad, text_value_weight_grad = (
        join_columns(b) for b in from_sub(text_weight_sum, 2)
    )
    gate_weight_grad, up_weight_grad = (join_hidden(b) for b in from_sub(ffn_weight_sum, 2))
    out_weight_grad = lax.ppermute(
        out_weight_sum, BOTH, [(b, a) for a, b in out_move]
    ).astype(f32)
    return (
        block_out,
        video_grad,
        caption_grad,
        cond_grad,
        ada_weight_grad,
        ada_bias_grad,
        query_weight_grad,
        key_weight_grad,
        value_weight_grad,
        out_weight_grad,
        text_key_weight_grad,
        text_value_weight_grad,
        gate_weight_grad,
        up_weight_grad,
        down_weight_grad,
        own_gains[0],
        own_gains[4],
        own_gains[5],
        own_gains[6],
        own_gains[1],
        own_gains[2],
        own_gains[3],
        gate_sum,
    )


def solution(mesh):
    placed = (
        P(("seq", "sub"), None),
        P(),
        P("sub", None),
        P(),
        P(),
        P(("seq", "sub"), None),
        P(("seq", "sub"), None),
        P(("seq", "sub")),
        P(("seq", "sub"), None),
        P(("seq", "sub"), None),
        P(("seq", "sub"), None),
        P(("seq", "sub"), None),
        P(("seq", "sub"), None),
        P(("seq", "sub"), None),
        P(("seq", "sub"), None),
        P(("seq", "sub"), None),
        P(("seq", "sub"), None),
        P(("seq", "sub")),
        P(("seq", "sub")),
        P(("seq", "sub")),
        P(("seq", "sub")),
        P(("seq", "sub")),
        P(("seq", "sub")),
        P(("seq", "sub")),
        P(),
        P(("seq", "sub"), None),
    )
    return jax.shard_map(
        body,
        mesh=mesh,
        in_specs=placed,
        out_specs=(
            P(("seq", "sub"), None),
            P(("seq", "sub"), None),
            P("sub", None),
            P(),
            P(("seq", "sub"), None),
            P(("seq", "sub")),
            P(("seq", "sub"), None),
            P(("seq", "sub"), None),
            P(("seq", "sub"), None),
            P(("seq", "sub"), None),
            P(("seq", "sub"), None),
            P(("seq", "sub"), None),
            P(("seq", "sub"), None),
            P(("seq", "sub"), None),
            P(("seq", "sub"), None),
            P(("seq", "sub")),
            P(("seq", "sub")),
            P(("seq", "sub")),
            P(("seq", "sub")),
            P(("seq", "sub")),
            P(("seq", "sub")),
            P(("seq", "sub")),
            P(),
        ),
        check_vma=False,
    )
```
